1024 devices in a mesh: comp: 8 (over z_lo), tile: 128 (over z_hi, y, x, core).
Axes of the slice: x: 4, y: 4, z: 32 (z_hi: 4, z_lo: 8; z = z_hi * 8 + z_lo), core: 2. Of those that a mesh axis runs over, the one named last changes fastest.
Arguments:
- state: float32 [8, 16, 512, 3072], P('comp', None, 'tile'), may hold values from -6 to 6
- coupling: float32 [8, 512, 3072], P('comp', 'tile'), may hold values from -6 to 6
- land_mask: int32 [8, 512, 3072], P('comp', 'tile'), may hold values 0 or 1
- codes: int32 [8, 512, 3072], P('comp', 'tile'), may hold values from 0 to 3
- mixing: float32 [8, 16], P('comp'), may hold values from 0.1 to 0.19
- courant: float32 [8, 16], P('comp'), may hold values from 0.05 to 0.24
- matrices: float32 [8, 4, 16, 16], P('comp'), may hold values from -1.5 to 1.5
- weights: bfloat16 [8, 36864, 8, 128], P('comp', 'tile'), may hold values from 0 to 0.25
- sources: int32 [8, 36864], P('comp', 'tile'), may hold values from 0 to 95, as said below
- targets: int32 [8, 36864], P('comp', 'tile'), may hold values from 0 to 767, as said below
Outputs:
- new_state: float32 [8, 16, 512, 3072], P('comp', None, 'tile')
- new_coupling: float32 [8, 512, 3072], P('comp', 'tile')
The draws below stay inside these ranges and needn't reach their ends.
Inputs may be any that keep to these rules, and one draw needn't show every extreme that they name: `sources`: on every tile each of its 96 blocks is the source of exactly 3 of its margin blocks. An atmosphere tile of group a targets only blocks of group 3 * 8 / 4 + a // 3, each of them exactly 3 times; an ocean tile of group o targets every block of the groups 3 (o - 3 * 8 / 4) + j, j < 3, exactly once.
All inputs are finite; a program needn't handle non-finite values. No bound on the sum of `land_mask` on one device may be relied on, other than what follows from the above.
Results may differ from the reference program's by a relative error of at most 0.0011.
Values sent between devices are 32-bit elements; how exact they have to be, the bound alone decides.
A program may use at most 32 MiB of HBM per device.

```python
import jax
import jax.numpy as jnp
from jax import lax

RA = 4
W = 3072
BLOCK = 128
BAND = 8
SUBSTEPS = 2
INTERVALS = 2
BRANCHES = 4
NV = 16
MARGINS = 288
ROWS = 512
N_COMP = 8
N_TILE = 128


def margin_pairs(key):
    blocks_dev = RA * W // BLOCK
    span = 3 * blocks_dev
    air_count = 3 * N_COMP // 4
    keys = jax.random.split(key, N_COMP * N_TILE)
    owners = jnp.arange(N_COMP * N_TILE, dtype=jnp.int32) // N_TILE

    def one_tile(tile_key, group):
        first_key, second_key = jax.random.split(tile_key)
        base = jnp.arange(span, dtype=jnp.int32) % blocks_dev
        source_list = jax.random.permutation(first_key, base).astype(jnp.int32)
        shuffled = jax.random.permutation(second_key, span).astype(jnp.int32)
        air_target = (air_count + group // 3) * blocks_dev + shuffled % blocks_dev
        sea_target = (3 * (group - air_count) + shuffled // blocks_dev) * blocks_dev + shuffled % blocks_dev
        target_list = jnp.where(group < air_count, air_target, sea_target).astype(jnp.int32)
        return (source_list, target_list)
    source_all, target_all = jax.vmap(one_tile)(keys, owners)
    return (source_all.reshape(N_COMP, N_TILE * span), target_all.reshape(N_COMP, N_TILE * span))


def draw_sources(key, part):
    return margin_pairs(jax.random.fold_in(key, 7))[0]


def draw_targets(key, part):
    return margin_pairs(jax.random.fold_in(key, 7))[1]


def touch_ends(entries, key, least, top_value):
    extent = entries.shape
    place = [jax.random.randint(jax.random.fold_in(key, axis), (), 0, extent[axis]) for axis in range(len(extent))]
    entries = entries.at[tuple(place)].set(least)
    longest = extent.index(max(extent))
    place[longest] = (place[longest] + 1) % extent[longest]
    return entries.at[tuple(place)].set(top_value)


def level_of(rng, shape, shards, low, high):
    gain, own = 1.0, jax.random.fold_in(rng, 6)
    for position, shards_of in shards:
        heights = jnp.exp(jax.random.uniform(jax.random.fold_in(own, position), (shards_of,), jnp.float32, low / len(shards), high / len(shards)))
        gain = gain * jnp.repeat(heights, shape[position] // shards_of).reshape([-1 if axis == position else 1 for axis in range(len(shape))])
    return gain


def noise(rng, extent, spread, limit, cuts=(), held_as=jnp.bfloat16):
    factor_of = level_of(rng, extent, cuts, -0.22, 0.18) if cuts else 1.0
    values = jax.random.normal(rng, extent, jnp.float32) * spread * factor_of
    return jnp.minimum(jnp.maximum(values, -limit), limit).astype(held_as)


def setup_inputs(seed: int = 0) -> dict:
    seeds = jax.random.split(jax.random.key(seed), 11)
    state = noise(seeds[0], (N_COMP, NV, ROWS, W), 1.0, 6.0, ((0, 8), (2, 128)), jnp.float32)
    coupling = noise(seeds[1], (N_COMP, ROWS, W), 1.0, 6.0, ((0, 8), (1, 128)), jnp.float32)
    land_mask = touch_ends((jax.random.randint(seeds[2], (N_COMP, ROWS, W), 0, 4) < 3).astype(jnp.int32), jax.random.fold_in(seeds[2], 1), 0, 1)
    codes = touch_ends(jax.random.randint(seeds[3], (N_COMP, ROWS, W), 0, BRANCHES), jax.random.fold_in(seeds[3], 1), 0, BRANCHES - 1).astype(jnp.int32)
    mixing = jnp.clip(0.1 + 0.089999996 * jax.random.uniform(seeds[4], (N_COMP, NV), jnp.float32) ** level_of(seeds[4], (N_COMP, NV), ((0, 8),), -0.2, 0.2), 0.1, 0.19)
    courant = jnp.clip(0.05 + 0.19 * jax.random.uniform(seeds[5], (N_COMP, NV), jnp.float32) ** level_of(seeds[5], (N_COMP, NV), ((0, 8),), -0.2, 0.2), 0.05, 0.24)
    matrices = noise(seeds[6], (N_COMP, BRANCHES, NV, NV), 0.3, 1.5, ((0, 8),), jnp.float32)
    weights = jnp.clip(0.25 * jax.random.uniform(seeds[7], (N_COMP, N_TILE * MARGINS, BAND, BLOCK), jnp.float32) ** level_of(seeds[7], (N_COMP, N_TILE * MARGINS, BAND, BLOCK), ((0, 8), (1, 128)), -0.2, 0.2), 0.0, 0.25).astype(jnp.bfloat16)
    sources = draw_sources(jax.random.fold_in(seeds[10], 71), 0)
    targets = draw_targets(jax.random.fold_in(seeds[10], 71), 0)
    return dict(state=state, coupling=coupling, land_mask=land_mask, codes=codes, mixing=mixing, courant=courant, matrices=matrices, weights=weights, sources=sources, targets=targets)


EXCHANGE = 0.5
OCEAN_SHARE = 0.3


def remap_all(handed, weights, sources, targets):
    blocks_dev = RA * W // BLOCK
    slot_count = N_COMP * blocks_dev
    blocks = handed.reshape(N_COMP, N_TILE, blocks_dev, BLOCK).astype(jnp.bfloat16)
    group_weights = weights.reshape(N_COMP, N_TILE, MARGINS, BAND, BLOCK)
    group_sources = sources.reshape(N_COMP, N_TILE, MARGINS)
    group_targets = targets.reshape(N_COMP, N_TILE, MARGINS)

    def one_group(pieces):
        tile_blocks, tile_weights, tile_sources, tile_targets = pieces
        rows_index = jnp.arange(N_TILE, dtype=jnp.int32)[:, None]
        picked = tile_blocks[rows_index, tile_sources].astype(jnp.float32)
        shifted = jnp.stack([jnp.roll(picked, -offset, axis=2) for offset in range(BAND)], axis=2)
        contrib = jnp.sum(tile_weights.astype(jnp.float32) * shifted, axis=2)
        selector = (tile_targets[:, :, None] == jnp.arange(slot_count, dtype=jnp.int32)[None, None, :]).astype(jnp.float32)
        return jnp.einsum("pks,pki->psi", selector, contrib, precision=lax.Precision.HIGHEST)

    payload = lax.map(one_group, (blocks, group_weights, group_sources, group_targets))
    payload = payload.reshape(N_COMP, N_TILE, N_COMP, blocks_dev * BLOCK)
    received = jnp.sum(payload, axis=0)
    return jnp.transpose(received, (1, 0, 2)).reshape(N_COMP, N_TILE * RA, W)


def reference(state, coupling, land_mask, codes, mixing, courant, matrices, weights, sources, targets):
    air_group = jnp.arange(N_COMP, dtype=jnp.int32) < 3 * N_COMP // 4
    wet_cells = land_mask.astype(jnp.float32)
    mixing_rate = mixing[:, :, None, None]
    courant_rate = courant[:, :, None, None]
    evolved = state
    handed = coupling
    for interval in range(INTERVALS):
        received = remap_all(handed, weights, sources, targets)
        surface = evolved[:, 0]
        surface_flux = wet_cells * EXCHANGE * (received - surface)
        new_surface = jnp.where(air_group[:, None, None], surface + surface_flux, surface - OCEAN_SHARE * received)
        diffused = evolved.at[:, 0].set(new_surface)
        for substep in range(SUBSTEPS):
            row_above = jnp.roll(diffused, 1, axis=2)
            row_below = jnp.roll(diffused, -1, axis=2)
            col_left = jnp.roll(diffused, 1, axis=3)
            col_right = jnp.roll(diffused, -1, axis=3)
            diffused = diffused + mixing_rate * (row_above + row_below + col_left + col_right - 4.0 * diffused) + courant_rate * (row_above - diffused)
        squashed = jnp.tanh(diffused)
        tendency = jnp.zeros_like(diffused)
        for branch in range(BRANCHES):
            branch_term = jnp.einsum("cij,cjrw->cirw", matrices[:, branch], squashed, precision=lax.Precision.HIGHEST)
            tendency = tendency + jnp.where(codes[:, None] == branch, branch_term, jnp.float32(0.0))
        evolved = diffused + tendency
        evolved = jnp.where(air_group[:, None, None, None], evolved, evolved * wet_cells[:, None])
        handed = jnp.where(air_group[:, None, None], surface_flux, evolved[:, 0])
    return evolved, handed
```

```python
import jax
import jax.numpy as jnp
from jax import lax
from jax.sharding import PartitionSpec as P

SUBSTEPS = 2
INTERVALS = 2
EXCHANGE = 0.5
OCEAN_SHARE = 0.3


def with_halo(cells, axis, dim, width):
    count = lax.axis_size(axis)
    head = lax.slice_in_dim(cells, 0, width, axis=dim)
    tail = lax.slice_in_dim(cells, cells.shape[dim] - width, cells.shape[dim], axis=dim)
    return jnp.concatenate(
        [
            lax.ppermute(tail, axis, [(i, (i + 1) % count) for i in range(count)]),
            cells,
            lax.ppermute(head, axis, [((i + 1) % count, i) for i in range(count)]),
        ],
        axis=dim,
    )


def advance_rows(padded, mixing_rate, courant_rate):
    center = padded[:, 1:-1]
    row_above = padded[:, :-2]
    row_below = padded[:, 2:]
    col_left = jnp.roll(center, 1, axis=2)
    col_right = jnp.roll(center, -1, axis=2)
    return (
        center
        + mixing_rate * (row_above + row_below + col_left + col_right - 4.0 * center)
        + courant_rate * (row_above - center)
    )


def remap_local(handed, weight_blocks, source_list, slot_list):
    block_width = weight_blocks.shape[-1]
    band_count = weight_blocks.shape[1]
    blocks = handed.reshape(-1, block_width).astype(jnp.bfloat16)
    picked = jnp.take(blocks, source_list, axis=0).astype(jnp.float32)
    shifted = jnp.stack([jnp.roll(picked, -offset, axis=1) for offset in range(band_count)], axis=1)
    contrib = jnp.sum(weight_blocks.astype(jnp.float32) * shifted, axis=1)
    selector = (slot_list[:, None] == jnp.arange(3 * blocks.shape[0], dtype=jnp.int32)[None, :]).astype(jnp.float32)
    payload = jnp.dot(selector.T, contrib, precision=lax.Precision.HIGHEST)
    return payload.reshape(3, -1)


def on_device(state, coupling, land_mask, codes, mixing, courant, matrices, weights, sources, targets):
    groups = lax.axis_size("comp")
    airs = 3 * groups // 4
    own_index = lax.axis_index("comp")
    air_group = own_index < airs
    evolved = state[0]
    handed = coupling[0]
    blocks_dev = handed.size // weights.shape[-1]
    first_group = jnp.where(air_group, airs + own_index // 3, 3 * (own_index - airs))
    slot_list = targets[0] - first_group * blocks_dev
    wet_cells = land_mask[0].astype(jnp.float32)
    mixing_rate = mixing[0][:, None, None]
    courant_rate = courant[0][:, None, None]
    physics_table = matrices[0]
    branch_index = jnp.arange(physics_table.shape[0], dtype=jnp.int32)[:, None, None]
    code_select = (codes[0][None] == branch_index).astype(jnp.float32)
    for interval in range(INTERVALS):
        payload = remap_local(handed, weights[0], sources[0], slot_list)
        parts = []
        for j in range(3):
            pairs = []
            for q in range(groups - airs):
                pairs += [(3 * q + j, airs + q), (airs + q, 3 * q + j)]
            sent = jnp.where(air_group, payload[0], payload[j])
            parts.append(lax.ppermute(sent, "comp", pairs))
        rest = with_halo(evolved[1:], "tile", 1, SUBSTEPS)
        received = (parts[0] + parts[1] + parts[2]).reshape(handed.shape)
        surface = evolved[0]
        surface_flux = wet_cells * EXCHANGE * (received - surface)
        coupled = jnp.where(air_group, surface + surface_flux, surface - OCEAN_SHARE * received)
        first = with_halo(coupled[None], "tile", 1, SUBSTEPS)
        diffused = jnp.concatenate([first, rest], axis=0)
        for substep in range(SUBSTEPS):
            diffused = advance_rows(diffused, mixing_rate, courant_rate)
        branch_terms = jnp.einsum(
            "bij,jrw->birw", physics_table, jnp.tanh(diffused), precision=lax.Precision.HIGHEST
        )
        evolved = diffused + jnp.einsum(
            "birw,brw->irw", branch_terms, code_select, precision=lax.Precision.HIGHEST
        )
        evolved = jnp.where(air_group, evolved, evolved * wet_cells[None])
        handed = jnp.where(air_group, surface_flux, evolved[0])
    return (evolved[None], handed[None])


def solution(mesh):
    placed = (
        P("comp", None, "tile", None),
        P("comp", "tile", None),
        P("comp", "tile", None),
        P("comp", "tile", None),
        P("comp", None),
        P("comp", None),
        P("comp", None, None, None),
        P("comp", "tile", None, None),
        P("comp", "tile"),
        P("comp", "tile"),
    )
    return jax.shard_map(
        on_device,
        mesh=mesh,
        in_specs=placed,
        out_specs=(P("comp", None, "tile", None), P("comp", "tile", None)),
        check_vma=False,
    )
```

```python
import functools

import jax
import jax.numpy as jnp
from jax import lax
from jax.experimental import pallas as pl
from jax.experimental.pallas import tpu as pltpu
from jax.sharding import PartitionSpec as P

SUBSTEPS = 2
INTERVALS = 2
EXCHANGE = 0.5
OCEAN_SHARE = 0.3

MESH = pl.DeviceIdType.MESH
LANES = 128
PLANE = 32
RELAYS = 12
FIRST_CHIP = 2
RELAY_AT_TARGET = False


def advance(above, center, below, mixing_rate, courant_rate):
    width = center.shape[1]
    left = pltpu.roll(center, 1, 1)
    right = pltpu.roll(center, width - 1, 1)
    return (
        center
        + mixing_rate * (above + below + left + right - 4.0 * center)
        + courant_rate * (above - center)
    )


def kernel(
    tiles, groups, widx, sidx, state, coupling, wet, codes, mask, mixing, courant, table, weights,
    out_state, out_coupling,
    x, y, z, d, shifted, payload, arrived, coupled, edge, relayed, surface, handed,
    p_send, p_recv, m_send, m_recv, s_send, c_recv, l_send, l_recv, f_send, f_recv,
):
    rows, fields, width = state.shape
    per_row = width // LANES
    blocks = rows * per_row
    piece = width // RELAYS
    airs = 3 * groups // 4
    g = lax.axis_index("comp")
    t = lax.axis_index("tile")
    air = g < airs
    sea = g >= airs
    plane = t // PLANE
    local = t % PLANE
    core = local % 2
    chip = local // 2
    last = local == PLANE - 1
    first = local == 0
    relay = jnp.logical_and(chip >= FIRST_CHIP, chip < FIRST_CHIP + RELAYS)
    down = (t + 1) % tiles
    up = (t + tiles - 1) % tiles
    partner = airs + g // 3
    slot = g % 3
    first_air = 3 * (g - airs)

    def relay_of(step, which, k):
        return ((plane + step) * PLANE + tiles + 2 * (FIRST_CHIP + k) + which) % tiles

    if RELAY_AT_TARGET:
        last_relay = functools.partial(relay_of, 1, 0)
        first_relay = functools.partial(relay_of, -1, 1)
        last_feeder = functools.partial(relay_of, 0, 1)
        first_feeder = functools.partial(relay_of, 0, 0)
        relay_source = ((plane + 2 * core - 1) * PLANE + tiles + (PLANE - 1) * (1 - core)) % tiles
        relay_target = plane * PLANE + (PLANE - 1) * core
        relay_row = (rows + 2) * core
    else:
        last_relay = functools.partial(relay_of, 0, 1)
        first_relay = functools.partial(relay_of, 0, 0)
        last_feeder = functools.partial(relay_of, 1, 0)
        first_feeder = functools.partial(relay_of, -1, 1)
        relay_source = plane * PLANE + (PLANE - 1) * core
        relay_target = ((plane + 2 * core - 1) * PLANE + tiles + (PLANE - 1) * (1 - core)) % tiles
        relay_row = (rows + 2) * (1 - core)
    relay_column = pl.multiple_of(jnp.clip(chip - FIRST_CHIP, 0, RELAYS - 1) * piece, LANES)
    relay_index = jnp.clip(chip - FIRST_CHIP, 0, RELAYS - 1)

    def remote(src, dst, send, recv, device):
        return pltpu.make_async_remote_copy(
            src_ref=src, dst_ref=dst, send_sem=send, recv_sem=recv, device_id=device, device_id_type=MESH
        )

    barrier = pltpu.get_barrier_semaphore()

    def greet(device):
        pl.semaphore_signal(barrier, inc=1, device_id=device, device_id_type=MESH)

    greet((g, up))
    greet((g, down))

    @pl.when(air)
    def _():
        greet((partner, t))

    @pl.when(sea)
    def _():
        for j in range(3):
            greet((first_air + j, t))

    @pl.when(relay)
    def _():
        greet((g, relay_source))

    @pl.when(last)
    def _():
        for k in range(RELAYS):
            greet((g, last_feeder(k)))

    @pl.when(first)
    def _():
        for k in range(RELAYS):
            greet((g, first_feeder(k)))

    def air_copy(it):
        return remote(payload.at[it, 0], arrived.at[it, slot], p_send.at[it, 0], p_recv.at[it, slot], (partner, t))

    def sea_copy(it, j):
        return remote(payload.at[it, j], arrived.at[it, 0], p_send.at[it, j], p_recv.at[it, 0], (first_air + j, t))

    def air_arrival(it):
        return remote(payload.at[it, 0], arrived.at[it, 0], p_send.at[it, 0], p_recv.at[it, 0], (partner, t))

    def sea_arrival(it, j):
        return remote(payload.at[it, j], arrived.at[it, j], p_send.at[it, j], p_recv.at[it, j], (first_air + j, t))

    def own_rows(it, start):
        if it == 0:
            return state.at[pl.ds(start, 2)]
        return x.at[it, pl.ds(start + 2, 2)]

    def own_piece(it, start, k):
        if it == 0:
            return state.at[pl.ds(start, 2), :, pl.ds(k * piece, piece)]
        return x.at[it, pl.ds(start + 2, 2), :, pl.ds(k * piece, piece)]

    def down_copy(it):
        return remote(own_rows(it, rows - 2), x.at[it, pl.ds(0, 2)], m_send.at[it, 0], m_recv.at[it, 0], (g, down))

    def up_copy(it):
        return remote(own_rows(it, 0), x.at[it, pl.ds(rows + 2, 2)], m_send.at[it, 1], m_recv.at[it, 1], (g, up))

    def last_piece(it, k):
        return remote(own_piece(it, rows - 2, k), relayed.at[it], s_send.at[it, k], l_recv.at[it], (g, last_relay(k)))

    def first_piece(it, k):
        return remote(own_piece(it, 0, k), relayed.at[it], s_send.at[it, k], l_recv.at[it], (g, first_relay(k)))

    def relay_copy(it):
        return remote(
            relayed.at[it],
            x.at[it, pl.ds(relay_row, 2), :, pl.ds(relay_column, piece)],
            l_send.at[it],
            c_recv.at[it, relay_index],
            (g, relay_target),
        )

    def relay_arrival(it):
        return remote(relayed.at[it], relayed.at[it], l_send.at[it], l_recv.at[it], (g, relay_target))

    def piece_arrival(it, start, k):
        dst = x.at[it, pl.ds(start, 2), :, pl.ds(k * piece, piece)]
        return remote(dst, dst, s_send.at[it, k], c_recv.at[it, k], (g, up))

    def edge_down(it):
        return remote(
            coupled.at[it, pl.ds((rows - 2) * per_row, 2 * per_row)], edge.at[it, 0], f_send.at[it, 0], f_recv.at[it, 0],
            (g, down),
        )

    def edge_up(it):
        return remote(
            coupled.at[it, pl.ds(0, 2 * per_row)], edge.at[it, 1], f_send.at[it, 1], f_recv.at[it, 1], (g, up)
        )

    def remap(cells, it):
        band = lax.broadcasted_iota(jnp.int32, (8, LANES), 0)

        def shift_group(n, _):
            start = pl.multiple_of(n * 8, 8)
            held = cells[pl.ds(start, 8), :].astype(jnp.bfloat16).astype(jnp.float32)
            for b in range(8):
                row = jnp.broadcast_to(held[b : b + 1], (8, LANES))
                for amount in (1, 2, 4):
                    row = jnp.where((band & amount) != 0, pltpu.roll(row, LANES - amount, 1), row)
                shifted[start + b] = row
            return 0

        lax.fori_loop(0, blocks // 8, shift_group, 0)

        def weigh_group(n, _):
            base = n * 8
            sums = []
            for b in range(8):
                product = weights[widx[base + b]].astype(jnp.float32) * shifted[sidx[base + b]]
                sums.append(jnp.sum(product, axis=0, keepdims=True))
            q = n // (blocks // 8)
            start = pl.multiple_of((n % (blocks // 8)) * 8, 8)
            payload[it, q, pl.ds(start, 8), :] = jnp.concatenate(sums, axis=0)
            return 0

        lax.fori_loop(0, 3 * blocks // 8, weigh_group, 0)

    def send_payload(it, of_air):
        if of_air:
            payload[it, 0] = payload[it, 0] + payload[it, 1] + payload[it, 2]
            air_copy(it).start()
        else:
            for j in range(3):
                sea_copy(it, j).start()

    def send_rows(it):
        @pl.when(jnp.logical_not(last))
        def _():
            down_copy(it).start()

        @pl.when(jnp.logical_not(first))
        def _():
            up_copy(it).start()

        @pl.when(last)
        def _():
            for k in range(RELAYS):
                last_piece(it, k).start()

        @pl.when(first)
        def _():
            for k in range(RELAYS):
                first_piece(it, k).start()

    def to_surface(it):
        def body(r, _):
            for c in range(per_row):
                surface[pl.ds(r * per_row + c, 1), :] = x[it, r + 2, 0:1, c * LANES : (c + 1) * LANES]
            return 0

        lax.fori_loop(0, rows, body, 0)

    def spread(source, base, row):
        for c in range(per_row):
            z[row, :, c * LANES : (c + 1) * LANES] = source[pl.ds(base + c, 1), :]

    for r in range(rows):
        x[0, r + 2] = state[r]
    remap(coupling, 0)
    to_surface(0)

    peers = (
        2
        + jnp.where(air, 1, 3)
        + jnp.where(relay, 1, 0)
        + jnp.where(jnp.logical_or(first, last), RELAYS, 0)
    )
    pl.semaphore_wait(barrier, peers)

    @pl.when(air)
    def _():
        send_payload(0, True)

    @pl.when(sea)
    def _():
        send_payload(0, False)

    send_rows(0)

    mixing_rate = jnp.broadcast_to(mixing[...], (fields, width))
    courant_rate = jnp.broadcast_to(courant[...], (fields, width))
    head = lax.broadcasted_iota(jnp.int32, (fields, width), 0) == 0
    chunk = 512 if width % 512 == 0 else width
    chunks = width // chunk

    for it in range(INTERVALS):
        final = it == INTERVALS - 1

        @pl.when(relay)
        def _():
            relay_arrival(it).wait_recv()
            relay_copy(it).start()

        @pl.when(air)
        def _():
            air_arrival(it).wait_recv()
            flux = wet[...] * EXCHANGE * (arrived[it, 0] - surface[...])
            handed[...] = flux
            coupled[it] = surface[...] + flux

        @pl.when(sea)
        def _():
            for j in range(3):
                sea_arrival(it, j).wait_recv()
            received = arrived[it, 0] + arrived[it, 1] + arrived[it, 2]
            coupled[it] = surface[...] - OCEAN_SHARE * received

        edge_down(it).start()
        edge_up(it).start()

        if not final:

            @pl.when(air)
            def _():
                remap(handed, it + 1)
                send_payload(it + 1, True)

        def own_row(r, _):
            spread(coupled.at[it], r * per_row, r + 2)
            return 0

        lax.fori_loop(0, rows, own_row, 0)

        @pl.when(jnp.logical_not(first))
        def _():
            down_copy(it).wait_recv()

        @pl.when(jnp.logical_not(last))
        def _():
            up_copy(it).wait_recv()

        @pl.when(first)
        def _():
            for k in range(RELAYS):
                piece_arrival(it, 0, k).wait_recv()

        @pl.when(last)
        def _():
            for k in range(RELAYS):
                piece_arrival(it, rows + 2, k).wait_recv()

        edge_down(it).wait_recv()
        edge_up(it).wait_recv()
        for r in range(2):
            spread(edge.at[it, 0], r * per_row, r)
            spread(edge.at[it, 1], r * per_row, rows + 2 + r)

        def first_substep(i, _):
            near = [jnp.where(head, jnp.broadcast_to(z[i + n], (fields, width)), x[it, i + n]) for n in range(3)]
            y[i] = advance(*near, mixing_rate, courant_rate)
            return 0

        lax.fori_loop(0, rows + 2, first_substep, 0)

        def second_substep(i, _):
            d[i] = advance(y[i], y[i + 1], y[i + 2], mixing_rate, courant_rate)
            return 0

        lax.fori_loop(0, rows, second_substep, 0)

        def physics(n, _):
            r = n // chunks
            cells = pl.ds(pl.multiple_of((n % chunks) * chunk, LANES), chunk)
            before = d[r, :, cells]
            squashed = jnp.tanh(before)
            high = squashed.astype(jnp.bfloat16)
            low = (squashed - high.astype(jnp.float32)).astype(jnp.bfloat16)
            terms = jnp.dot(table[...], jnp.concatenate([high, low, high], axis=0), preferred_element_type=jnp.float32)
            code = jnp.broadcast_to(codes[r, :, cells], (fields, chunk))
            tendency = jnp.where(
                code < 2,
                jnp.where(code == 0, terms[:fields], terms[fields : 2 * fields]),
                jnp.where(code == 2, terms[2 * fields : 3 * fields], terms[3 * fields :]),
            )
            after = (before + tendency) * mask[r, :, cells]
            if final:
                out_state[r, :, cells] = after
            else:
                x[it + 1, r + 2, :, cells] = after
            return 0

        lax.fori_loop(0, rows * chunks, physics, 0)

        if not final:
            to_surface(it + 1)

            @pl.when(sea)
            def _():
                remap(surface, it + 1)
                send_payload(it + 1, False)

            send_rows(it + 1)
        else:

            @pl.when(air)
            def _():
                out_coupling[...] = handed[...]

            @pl.when(sea)
            def _():
                def body(r, _):
                    for c in range(per_row):
                        out_coupling[pl.ds(r * per_row + c, 1), :] = out_state[r, 0:1, c * LANES : (c + 1) * LANES]
                    return 0

                lax.fori_loop(0, rows, body, 0)

    for it in range(INTERVALS):

        @pl.when(air)
        def _():
            air_copy(it).wait_send()

        @pl.when(sea)
        def _():
            for j in range(3):
                sea_copy(it, j).wait_send()

        @pl.when(relay)
        def _():
            relay_copy(it).wait_send()

        @pl.when(jnp.logical_not(last))
        def _():
            down_copy(it).wait_send()

        @pl.when(jnp.logical_not(first))
        def _():
            up_copy(it).wait_send()

        @pl.when(last)
        def _():
            for k in range(RELAYS):
                last_piece(it, k).wait_send()

        @pl.when(first)
        def _():
            for k in range(RELAYS):
                first_piece(it, k).wait_send()

        edge_down(it).wait_send()
        edge_up(it).wait_send()


def on_device(tiles, groups, state, coupling, land_mask, codes, mixing, courant, matrices, weights, sources, targets):
    airs = 3 * groups // 4
    own_index = lax.axis_index("comp")
    air_group = own_index < airs
    fields, rows, width = state.shape[1:]
    branches = matrices.shape[1]
    blocks = rows * width // LANES
    margins = sources.shape[1]

    first_group = jnp.where(air_group, airs + own_index // 3, 3 * (own_index - airs))
    slots = targets[0] - first_group * blocks
    number = jnp.arange(margins, dtype=jnp.int32)
    earlier = jnp.logical_and(slots[None, :] == slots[:, None], number[None, :] < number[:, None])
    place = slots + blocks * jnp.sum(earlier.astype(jnp.int32), axis=1)
    chosen = place[None, :] == number[:, None]
    widx = jnp.sum(jnp.where(chosen, number[None, :], 0), axis=1)
    sidx = jnp.sum(jnp.where(chosen, sources[0][None, :], 0), axis=1)

    wet = land_mask[0].astype(jnp.float32)
    mask = jnp.where(air_group, 1.0, wet)
    stacked = matrices[0].reshape(branches * fields, fields)
    high = lax.reduce_precision(stacked, 8, 7)
    low = lax.reduce_precision(stacked - high, 8, 7)
    table = jnp.concatenate([high, high, low], axis=1).astype(jnp.bfloat16)

    vmem = pl.BlockSpec(memory_space=pltpu.VMEM)
    smem = pl.BlockSpec(memory_space=pltpu.SMEM)
    f32 = jnp.float32
    dma = pltpu.SemaphoreType.DMA
    n = INTERVALS
    new_state, new_coupling = pl.pallas_call(
        functools.partial(kernel, tiles, groups),
        out_shape=(
            jax.ShapeDtypeStruct((rows, fields, width), f32),
            jax.ShapeDtypeStruct((blocks, LANES), f32),
        ),
        in_specs=[smem, smem] + [vmem] * 9,
        out_specs=(vmem, vmem),
        scratch_shapes=[
            pltpu.VMEM((n, rows + 4, fields, width), f32),
            pltpu.VMEM((rows + 2, fields, width), f32),
            pltpu.VMEM((rows + 4, 1, width), f32),
            pltpu.VMEM((rows, fields, width), f32),
            pltpu.VMEM((blocks, 8, LANES), f32),
            pltpu.VMEM((n, 3, blocks, LANES), f32),
            pltpu.VMEM((n, 3, blocks, LANES), f32),
            pltpu.VMEM((n, blocks, LANES), f32),
            pltpu.VMEM((n, 2, 2 * width // LANES, LANES), f32),
            pltpu.VMEM((n, 2, fields, width // RELAYS), f32),
            pltpu.VMEM((blocks, LANES), f32),
            pltpu.VMEM((blocks, LANES), f32),
            dma((n, 3)),
            dma((n, 3)),
            dma((n, 2)),
            dma((n, 2)),
            dma((n, RELAYS)),
            dma((n, RELAYS)),
            dma((n,)),
            dma((n,)),
            dma((n, 2)),
            dma((n, 2)),
        ],
        compiler_params=pltpu.CompilerParams(collective_id=0, has_side_effects=True, vmem_limit_bytes=48 << 20),
        name="coupled_step",
    )(
        widx,
        sidx,
        jnp.transpose(state[0], (1, 0, 2)),
        coupling[0].reshape(blocks, LANES),
        wet.reshape(blocks, LANES),
        codes[0].reshape(rows, 1, width),
        mask.reshape(rows, 1, width),
        mixing[0][:, None],
        courant[0][:, None],
        table,
        weights[0],
    )
    return jnp.transpose(new_state, (1, 0, 2))[None], new_coupling.reshape(rows, width)[None]


def solution(mesh):
    placed = (
        P("comp", None, "tile", None),
        P("comp", "tile", None),
        P("comp", "tile", None),
        P("comp", "tile", None),
        P("comp", None),
        P("comp", None),
        P("comp", None, None, None),
        P("comp", "tile", None, None),
        P("comp", "tile"),
        P("comp", "tile"),
    )
    return jax.shard_map(
        functools.partial(on_device, mesh.shape["tile"], mesh.shape["comp"]),
        mesh=mesh,
        in_specs=placed,
        out_specs=(P("comp", None, "tile", None), P("comp", "tile", None)),
        check_vma=False,
    )
```
